512 devices in a mesh: blk: 32 (over z, core), env: 16 (over y, x).
Axes of the slice: x: 4, y: 4, z: 16, core: 2. Of those that a mesh axis runs over, the one named last changes fastest.
Arguments:
- psi: float32 [4096, 1024], P('blk', 'env')
- env_left: bfloat16 [4096, 16, 1024], P('blk', 'env')
- env_right: bfloat16 [16, 1024, 1024], P('env')
- sector_tiles: int32 [16], replicated, may hold values from 1 to 8, as said below
- pairing: int32 [16, 16], replicated, may hold values from 0 to 15, as said below
- coupling: int32 [16, 16], replicated, may hold values from 0 to 1, as said below
Outputs:
- products: float32 [3, 4096, 1024], P(None, 'blk', 'env')
- quotients: float32 [3], replicated
- next_vector: float32 [4096, 1024], P('blk', 'env')
The draws below stay inside these ranges and needn't reach their ends.
Inputs may be any that keep to these rules, and one draw needn't show every extreme that they name: Sector k covers tiles first_tile[k] to first_tile[k] + sector_tiles[k] - 1 of 128 rows; together the sectors cover all 32 tiles. Channel 0 maps every sector to itself: pairing[k, 0] = k. Channel 0 acts on every sector: coupling[k, 0] = 1.
All inputs are finite; a program needn't handle non-finite values.
Results may differ from the reference program's by a relative error of at most 0.0091.
Values may be sent and summed in bfloat16 or wider, within the bound.
No kernel may reach another device: no remote copies, remote signals or barrier semaphores. Data moves between devices by JAX's collectives and lax.ppermute only.
A program may use at most 64 MiB of HBM per device.

```python
import jax
import jax.numpy as jnp
from jax import lax

TILE = 128
TERMS = 16
RB = 1024
ITERS = 3
NT = 32
NR = 4096
NSEC = 16
SRCT = 8
SRCR = 1024


def sector_counts(key):
    sector_count = NT // 2
    place_key = jax.random.fold_in(key, 7001)
    fill_key = jax.random.fold_in(key, 7002)
    sector_ids = jnp.arange(sector_count, dtype=jnp.int32)
    largest_at = jax.random.randint(place_key, (), 0, sector_count, dtype=jnp.int32)
    start_counts = jnp.where(sector_ids == largest_at, SRCT, 1).astype(jnp.int32)
    extra_units = NT - SRCT - (sector_count - 1)

    def place_unit(unit_index, counts):
        scores = jax.random.randint(jax.random.fold_in(fill_key, unit_index), (sector_count,), 0, 1048576, dtype=jnp.int32)
        scores = scores * sector_count + sector_ids
        scores = jnp.where(counts < SRCT, scores, -1)
        chosen = jnp.argmax(scores).astype(jnp.int32)
        return counts + (sector_ids == chosen).astype(jnp.int32)
    return lax.fori_loop(0, extra_units, place_unit, start_counts)


def draw_sector_tiles(key, part):
    return sector_counts(key).astype(jnp.int32)


def draw_pairing(key, part):
    source_pick = jax.random.randint(jax.random.fold_in(key, 7007), (NSEC, TERMS), 0, NSEC, dtype=jnp.int32)
    channel_ids = jnp.arange(TERMS, dtype=jnp.int32)[None, :]
    sector_ids = jnp.arange(NSEC, dtype=jnp.int32)[:, None]
    return jnp.where(channel_ids == 0, sector_ids, source_pick).astype(jnp.int32)


def draw_coupling(key, part):
    levels = jax.random.randint(jax.random.fold_in(key, 7008), (NSEC, TERMS), 0, 4, dtype=jnp.int32)
    channel_ids = jnp.arange(TERMS, dtype=jnp.int32)[None, :]
    active = jnp.where(levels < 3, 1, 0)
    return jnp.where(channel_ids == 0, 1, active).astype(jnp.int32)


def draw_env_left(key, part):
    row_count = NT * TILE
    counts = sector_counts(key)
    first_tile = (jnp.cumsum(counts) - counts).astype(jnp.int32)
    tile_ids = jnp.arange(NT, dtype=jnp.int32)
    sector_of = (jnp.sum((tile_ids[:, None] >= first_tile[None, :]).astype(jnp.int32), axis=1) - 1).astype(jnp.int32)
    row_ids = jnp.arange(row_count, dtype=jnp.int32)
    tile_first_row = (TILE * first_tile[sector_of]).astype(jnp.int32)
    local_row = row_ids - tile_first_row[row_ids // TILE]
    noise_key = jax.random.fold_in(key, 7003)
    scale_key = jax.random.fold_in(key, 7004)
    draw_shape = (row_count, TERMS, SRCR)
    noise_part = jax.random.normal(noise_key, draw_shape)
    diag_scale = jnp.exp(jax.random.uniform(scale_key, (row_count,), minval=-0.7, maxval=0.7))
    channel_ids = jnp.arange(TERMS, dtype=jnp.int32)
    offsets = jnp.arange(SRCR, dtype=jnp.int32)
    on_diag = (channel_ids[None, :, None] == 0) & (offsets[None, None, :] == local_row[:, None, None])
    values = noise_part * SRCR ** (-0.5) + jnp.where(on_diag, diag_scale[:, None, None], 0.0)
    return values.astype(jnp.float32).astype(jnp.bfloat16)


def draw_env_right(key, part):
    noise_key = jax.random.fold_in(key, 7005)
    scale_key = jax.random.fold_in(key, 7006)
    draw_shape = (TERMS, RB, RB)
    noise_part = jax.random.normal(noise_key, draw_shape)
    column_scale = jnp.exp(jax.random.uniform(scale_key, (RB,), minval=-0.7, maxval=0.7))
    channel_ids = jnp.arange(TERMS, dtype=jnp.int32)
    column_ids = jnp.arange(RB, dtype=jnp.int32)
    on_diag = (channel_ids[:, None, None] == 0) & (column_ids[None, :, None] == column_ids[None, None, :])
    values = noise_part * (RB * TERMS) ** (-0.5) + jnp.where(on_diag, column_scale[None, None, :], 0.0)
    return values.astype(jnp.float32).astype(jnp.bfloat16)


def draw_psi(key, part):
    row_count = NT * TILE
    key_values, key_scale = jax.random.split(key, 2)
    row_place = jnp.arange(row_count, dtype=jnp.float32) / (row_count - 1)
    col_place = jnp.arange(RB, dtype=jnp.float32) / (RB - 1)
    growth = (1.0 + 2.0 * row_place)[:, None] * (1.0 + 2.0 * col_place)[None, :]
    roughness = jnp.exp(jax.random.uniform(key_scale, (row_count, 1), minval=-0.35, maxval=0.35))
    values = jax.random.normal(key_values, (row_count, RB))
    return (values * growth * roughness).astype(jnp.float32)


def setup_inputs(seed: int = 0) -> dict:
    key_of = jax.random.split(jax.random.key(seed), 7)
    psi = draw_psi(jax.random.fold_in(key_of[6], 71), 0)
    env_left = draw_env_left(jax.random.fold_in(key_of[6], 71), 0)
    env_right = draw_env_right(jax.random.fold_in(key_of[6], 71), 0)
    sector_tiles = draw_sector_tiles(jax.random.fold_in(key_of[6], 71), 0)
    pairing = draw_pairing(jax.random.fold_in(key_of[6], 71), 0)
    coupling = draw_coupling(jax.random.fold_in(key_of[6], 71), 0)
    return dict(psi=psi, env_left=env_left, env_right=env_right, sector_tiles=sector_tiles, pairing=pairing, coupling=coupling)


EPSILON = 1e-06

def reference(psi, env_left, env_right, sector_tiles, pairing, coupling):
    tile_counts = sector_tiles.astype(jnp.int32)
    first_tile = (jnp.cumsum(tile_counts) - tile_counts).astype(jnp.int32)
    tile_ids = jnp.arange(NT, dtype=jnp.int32)
    sector_of = (lax.optimization_barrier(jnp.sum((tile_ids[:, None] >= first_tile[None, :]).astype(jnp.int32), axis=1)) - 1).astype(jnp.int32)
    source_sector = pairing[sector_of].astype(jnp.int32)
    source_first = (first_tile[source_sector] * TILE).astype(jnp.int32)
    source_rows = (tile_counts[source_sector] * TILE).astype(jnp.int32)
    coupled = coupling[sector_of] == 1
    offsets = jnp.arange(SRCR, dtype=jnp.int32)
    keep_mask = (offsets[None, None, :] < source_rows[:, :, None]) & coupled[:, :, None]
    panels = jnp.where(keep_mask[:, None], env_left.reshape(NT, TILE, TERMS, SRCR), jnp.zeros((), jnp.bfloat16))
    right_wide = env_right.astype(jnp.float32)

    def apply_operator(vector):
        padded = jnp.concatenate([vector.astype(jnp.bfloat16), jnp.zeros((SRCR, RB), jnp.bfloat16)], axis=0)

        def one_tile(tile):
            starts = source_first[tile]
            source_slabs = jax.vmap(lambda first_row: lax.dynamic_slice_in_dim(padded, first_row, SRCR, 0))(starts)
            channel_mix = jnp.einsum('xtj,tjc->txc', panels[tile].astype(jnp.float32), source_slabs.astype(jnp.float32)).astype(jnp.bfloat16)
            return jnp.einsum('txb,tbc->xc', channel_mix.astype(jnp.float32), right_wide)
        return lax.map(one_tile, tile_ids).reshape(NR, RB)
    vector = psi
    product_list = []
    quotient_list = []
    for iteration in range(ITERS):
        product = apply_operator(vector)
        quotient = jnp.sum(vector * product) / jnp.sum(vector * vector)
        residual = product - quotient * vector
        energy = jnp.mean(residual * residual)
        vector = residual * lax.rsqrt(energy + EPSILON)
        product_list.append(product)
        quotient_list.append(quotient)
    return (jnp.stack(product_list), jnp.stack(quotient_list), vector)
```

```python
import functools

import jax
import jax.numpy as jnp
from jax import lax
from jax.experimental import pallas as pl
from jax.experimental.pallas import tpu as pltpu
from jax.sharding import Mesh
from jax.sharding import PartitionSpec as P

TILE = 128
HALF = TILE // 2
ITERS = 3
GROUP = 4

EPSILON = 1e-06

ENV = ("y", "x")
BF16 = jnp.bfloat16
F32 = jnp.float32


def lookup_sources(sector_tiles, pairing, coupling, tile_ids, source_span):
    first_tile = jnp.cumsum(sector_tiles) - sector_tiles
    sector_ids = jnp.arange(sector_tiles.shape[0], dtype=jnp.int32)
    sector_of = jnp.sum((tile_ids[:, None] >= first_tile[None, :]).astype(jnp.int32), axis=1) - 1
    sector_pick = (sector_of[:, None] == sector_ids[None, :]).astype(jnp.int32)
    source_sector = jnp.sum(sector_pick[:, :, None] * pairing[None, :, :], axis=1)
    coupled = jnp.sum(sector_pick[:, :, None] * coupling[None, :, :], axis=1)
    source_pick = (source_sector[:, :, None] == sector_ids[None, None, :]).astype(jnp.int32)
    source_first = jnp.sum(source_pick * first_tile[None, None, :], axis=2) * TILE
    source_rows = jnp.sum(source_pick * sector_tiles[None, None, :], axis=2) * TILE
    offsets = jnp.arange(source_span, dtype=jnp.int32)
    keep_mask = (offsets[None, None, :] < source_rows[:, :, None]) & (coupled[:, :, None] == 1)
    return (source_first, keep_mask)


def pack(block):
    return jnp.concatenate([block[:HALF], block[HALF:]], axis=1)


def unpack(packed):
    width = packed.shape[1] // 2
    return jnp.concatenate([packed[:, :width], packed[:, width:]], axis=0)


def operator_kernel(first, rows, width, *refs):
    if first:
        meta, w_ref, panel_ref, right_ref, out_ref, rows_scr, mix_scr, acc = refs
    else:
        meta, w_ref, p_ref, prev_ref, panel_ref, right_ref, out_ref, rows_scr, mix_scr, acc, q_scr = refs
    step = pl.program_id(0)
    tiles = rows // TILE
    span = panel_ref.shape[2]

    @pl.when(step == 0)
    def _():
        if first:
            d = w_ref[...]
        else:
            w = w_ref[...]
            p = p_ref[...]
            ww = jnp.sum(w * w, keepdims=True)
            wp = jnp.sum(w * p, keepdims=True)
            q = jnp.where(ww > 0, wp / jnp.where(ww > 0, ww, 1.0), 0.0)
            d = p - q * w
            rr = jnp.sum(d * d, keepdims=True)
            lane = lax.broadcasted_iota(jnp.int32, (8, 2 * width), 1)
            q_scr[...] = jnp.where(
                lane == 0, ww, jnp.where(lane == 1, wp, jnp.where(lane == 2, rr, q))
            )
        u = d.astype(BF16)
        core = meta[meta.shape[0] - 1]
        for side in range(2):
            for z in range(tiles // 2):
                block = u[(side * (tiles // 2) + z) * HALF : (side * (tiles // 2) + z + 1) * HALF]
                parity = core if side == 0 else 1 - core
                start = pl.multiple_of((2 * z + parity) * TILE, TILE)
                rows_scr[pl.ds(start, HALF), :] = block[:, :width]
                rows_scr[pl.ds(start + HALF, HALF), :] = block[:, width:]
        rows_scr[pl.ds(rows, span), :] = jnp.zeros((span, width), BF16)
        acc[...] = jnp.zeros_like(acc)

    for i in range(GROUP):
        start = pl.multiple_of(meta[step * GROUP + i], TILE)
        slab = rows_scr[pl.ds(start, span), :]
        mixed = jnp.dot(panel_ref[i], slab, preferred_element_type=F32)
        mix_scr[:, i * width : (i + 1) * width] = mixed.astype(BF16)
    acc[...] += jnp.dot(mix_scr[...], right_ref[...], preferred_element_type=F32)

    @pl.when(step == pl.num_programs(0) - 1)
    def _():
        for e in range(out_ref.shape[0]):
            cols = acc[:, e * width : (e + 1) * width]
            packed = jnp.concatenate([cols[:HALF], cols[HALF:]], axis=1)
            if first:
                out_ref[e, pl.ds(0, HALF), :] = packed
                out_ref[e, pl.ds(HALF, 8), :] = jnp.zeros((8, 2 * width), F32)
            else:
                q = q_scr[0:1, 3:4]
                out_ref[e, pl.ds(0, HALF), :] = packed + q * prev_ref[e]
                out_ref[e, pl.ds(HALF, 8), :] = q_scr[...]


def apply_operator(meta, w, p, prev, panels, right):
    first = p is None
    channels, tile, span = panels.shape
    full = right.shape[1]
    env_count = channels
    width = full // env_count
    rows = w.shape[0] * 2
    whole = lambda shape: pl.BlockSpec(shape, lambda g, m: (0,) * len(shape))
    in_specs = [whole(w.shape)]
    args = [w]
    if not first:
        in_specs += [whole(p.shape), whole(prev.shape)]
        args += [p, prev]
    in_specs += [
        pl.BlockSpec((GROUP, tile, span), lambda g, m: (g, 0, 0)),
        pl.BlockSpec((GROUP * width, full), lambda g, m: (g, 0)),
    ]
    args += [panels, right]
    scratch = [
        pltpu.VMEM((rows + span, width), BF16),
        pltpu.VMEM((tile, GROUP * width), BF16),
        pltpu.VMEM((tile, full), F32),
    ]
    if not first:
        scratch.append(pltpu.VMEM((8, 2 * width), F32))
    out_shape = (env_count, HALF + 8, 2 * width)
    return pl.pallas_call(
        functools.partial(operator_kernel, first, rows, width),
        grid_spec=pltpu.PrefetchScalarGridSpec(
            num_scalar_prefetch=1,
            grid=(channels // GROUP,),
            in_specs=in_specs,
            out_specs=whole(out_shape),
            scratch_shapes=scratch,
        ),
        out_shape=jax.ShapeDtypeStruct(out_shape, F32),
        compiler_params=pltpu.CompilerParams(
            dimension_semantics=("arbitrary",), vmem_limit_bytes=48 * 1024 * 1024
        ),
        cost_estimate=pl.CostEstimate(
            flops=4 * channels * tile * span * width,
            bytes_accessed=panels.size * 2 + right.size * 2 + 3 * 1024 * 1024,
            transcendentals=0,
        ),
        name="operator_first" if first else "operator_next",
    )(meta, *args)


def merge(ww, wp, rr, q):
    ww_all = jnp.sum(ww)
    wp_all = jnp.sum(wp)
    q_all = wp_all / ww_all
    spread = (q - q_all) * jnp.sqrt(ww)
    rr_all = jnp.sum(rr) + jnp.sum(spread * spread)
    return ww_all, wp_all, rr_all, q_all


def gather_rows(packed):
    own = lax.all_gather(packed, "z", axis=0, tiled=True)
    other = lax.ppermute(own, "c", [(0, 1), (1, 0)])
    return jnp.concatenate([own, other], axis=0)


def per_device(psi, env_left, env_right, sector_tiles, pairing, coupling):
    tile, width = psi.shape
    env_count = lax.axis_size(ENV)
    row_count = tile * lax.axis_size(("z", "c"))
    source_span = env_left.shape[2]
    full_width = width * env_count
    entry_count = float(row_count * full_width)
    core = lax.axis_index("c")
    tile_ids = lax.axis_index(("z", "c")).reshape(1)
    source_first, keep_mask = lookup_sources(
        sector_tiles, pairing, coupling, tile_ids, source_span
    )
    meta = jnp.concatenate([source_first.reshape(-1), core.reshape(1)]).astype(jnp.int32)
    local_keep = lax.dynamic_slice_in_dim(keep_mask, lax.axis_index(ENV), 1, 1)
    left_panel = jnp.where(local_keep[0], env_left.reshape(tile, source_span), 0)
    panels = lax.all_gather(left_panel, ENV, axis=0)
    right = lax.all_to_all(
        env_right.reshape(env_count, width, full_width), ENV, 0, 0, tiled=True
    ).reshape(env_count * width, full_width)

    own_w = pack(psi)
    w = gather_rows(own_w)
    sent = apply_operator(meta, w, None, None, panels, right)
    partial = sent[:, :HALF]
    arrived = lax.all_to_all(sent, ENV, 0, 0, tiled=True)
    own_p = jnp.sum(arrived[:, :HALF], axis=0)
    product_list = [own_p]
    quotient_list = []
    for iteration in range(1, ITERS):
        p = gather_rows(own_p)
        sent = apply_operator(meta, w, p, partial, panels, right)
        arrived = lax.all_to_all(sent, ENV, 0, 0, tiled=True)
        notes = arrived[:, HALF]
        _, _, energy, q = merge(notes[:, 0], notes[:, 1], notes[:, 2], notes[:, 3])
        scale = lax.rsqrt(energy / entry_count + EPSILON)
        next_p = scale * (jnp.sum(arrived[:, :HALF], axis=0) - q * own_p)
        own_w = scale * (own_p - q * own_w)
        if iteration < ITERS - 1:
            partial = scale * (sent[:, :HALF] - q * partial)
            w = scale * (p - q * w)
        own_p = next_p
        product_list.append(own_p)
        quotient_list.append(q)

    ww = jnp.sum(own_w * own_w)
    wp = jnp.sum(own_w * own_p)
    q = jnp.where(ww > 0, wp / jnp.where(ww > 0, ww, 1.0), 0.0)
    d = own_p - q * own_w
    rr = jnp.sum(d * d)
    lane = lax.broadcasted_iota(jnp.int32, (8, TILE), 1)

    def note(ww, wp, rr, q):
        return jnp.where(lane == 0, ww, jnp.where(lane == 1, wp, jnp.where(lane == 2, rr, q)))

    def exchange(values, axes):
        count = lax.axis_size(axes)
        sent = jnp.broadcast_to(note(*values)[None], (count, 8, TILE))
        got = lax.all_to_all(sent, axes, 0, 0, tiled=True)[:, 0]
        return merge(got[:, 0], got[:, 1], got[:, 2], got[:, 3])

    values = (ww, wp, rr, q)
    for axes in ("c", ENV, "z"):
        values = exchange(values, axes)
    _, _, energy, q = values
    quotient_list.append(q)
    scale = lax.rsqrt(energy / entry_count + EPSILON)
    own_w = scale * (own_p - q * own_w)
    products = jnp.stack([unpack(x) for x in product_list])
    return (products, jnp.stack(quotient_list), unpack(own_w))


def solution(mesh):
    shape = mesh.devices.shape
    fine = Mesh(mesh.devices.reshape(shape[0] // 2, 2, 4, shape[1] // 4), ("z", "c", "y", "x"))
    blk = ("z", "c")
    placed = (P(blk, ENV), P(blk, ENV, None), P(ENV, None, None), P(), P(), P())
    return jax.shard_map(
        per_device,
        mesh=fine,
        in_specs=placed,
        out_specs=(P(None, blk, ENV), P(), P(blk, ENV)),
        check_vma=False,
    )
```

```python
import functools

import jax
import jax.numpy as jnp
from jax import lax
from jax.experimental import pallas as pl
from jax.experimental.pallas import tpu as pltpu
from jax.sharding import Mesh
from jax.sharding import PartitionSpec as P

TILE = 128
HALF = TILE // 2
ITERS = 3
GROUP = 4
NOTE = 8

EPSILON = 1e-06

ENV = ("y", "x")
BF16 = jnp.bfloat16
F32 = jnp.float32
PARAMS = dict(vmem_limit_bytes=48 * 1024 * 1024)


def lanes_of(*values):
    lane = lax.broadcasted_iota(jnp.int32, (NOTE, TILE), 1)
    out = jnp.zeros((NOTE, TILE), F32)
    for i, value in enumerate(values):
        out = jnp.where(lane == i, value, out)
    return out


def total(x):
    return jnp.sum(x, keepdims=True)


def own_sums(w, p):
    ww = total(w * w)
    wp = total(w * p)
    q = jnp.where(ww > 0, wp / jnp.where(ww > 0, ww, 1.0), 0.0)
    d = p - q * w
    return d, (ww, wp, total(d * d), q)


def merge(notes):
    ww, wp, rr, q = (notes[:, i : i + 1] for i in range(4))
    ww_all, wp_all = total(ww), total(wp)
    q_all = wp_all / ww_all
    spread = (q - q_all) * jnp.sqrt(ww)
    return ww_all, wp_all, total(rr) + total(spread * spread), q_all


def pack(block):
    return jnp.concatenate([block[:HALF], block[HALF:]], axis=1)


def unpack(packed):
    width = packed.shape[1] // 2
    return jnp.concatenate([packed[:, :width], packed[:, width:]], axis=0)


def smem():
    return pl.BlockSpec(memory_space=pltpu.SMEM)


def vmem():
    return pl.BlockSpec(memory_space=pltpu.VMEM)


def prepare_kernel(place, tiles_ref, pair_ref, couple_ref, left_ref, psi_ref,
                   meta_ref, panel_ref, packed_ref, first):
    sectors, channels = pair_ref.shape
    mine, core, channel = place[0], place[1], place[2]

    def place_sector(k, carry):
        start, sector = carry
        first[k] = start
        sector = jnp.where(start <= mine, k, sector)
        return start + tiles_ref[k], sector

    _, sector = lax.fori_loop(0, sectors, place_sector, (0, 0))
    for t in range(channels):
        meta_ref[t] = first[pair_ref[sector, t]] * TILE
    meta_ref[channels] = core
    source = pair_ref[sector, channel]
    count = jnp.where(couple_ref[sector, channel] == 1, tiles_ref[source] * TILE, 0)
    column = lax.broadcasted_iota(jnp.int32, left_ref.shape, 1)
    panel_ref[...] = jnp.where(column < count, left_ref[...], jnp.zeros((), BF16))
    packed_ref[...] = pack(psi_ref[...])


def prepare(place, sector_tiles, pairing, coupling, left, psi):
    channels = pairing.shape[1]
    return pl.pallas_call(
        prepare_kernel,
        in_specs=[smem()] * 4 + [vmem()] * 2,
        out_specs=[smem(), vmem(), vmem()],
        out_shape=[
            jax.ShapeDtypeStruct((channels + 1,), jnp.int32),
            jax.ShapeDtypeStruct(left.shape, BF16),
            jax.ShapeDtypeStruct((psi.shape[0] // 2, psi.shape[1] * 2), F32),
        ],
        scratch_shapes=[pltpu.SMEM(sector_tiles.shape, jnp.int32)],
        compiler_params=pltpu.CompilerParams(**PARAMS),
        name="prepare",
    )(place, sector_tiles, pairing, coupling, left, psi)


def operator_kernel(turn, rows, width, *refs):
    refs = list(refs)
    meta = refs.pop(0)
    vectors = [(refs.pop(0), refs.pop(0)) for _ in range(turn + 1)]
    earlier = [refs.pop(0) for _ in range(turn)]
    note_ref = refs.pop(0) if turn == 2 else None
    panel_ref, right_ref, out_ref, rows_scr, mix_scr, acc, note_scr = refs
    step = pl.program_id(0)
    pairs = rows // TILE // 2
    span = panel_ref.shape[2]

    @pl.when(step == 0)
    def _():
        def both(index):
            return [ref[...] for ref in vectors[index]]

        if turn == 0:
            d = both(0)
        else:
            w, p = both(0), both(1)
            if turn == 2:
                q0, s0 = note_ref[0:1, 0:1], note_ref[0:1, 1:2]
                w = [s0 * (b - q0 * a) for a, b in zip(w, p)]
                p = both(2)
            ww = total(w[0] * w[0] + w[1] * w[1])
            wp = total(w[0] * p[0] + w[1] * p[1])
            q = jnp.where(ww > 0, wp / jnp.where(ww > 0, ww, 1.0), 0.0)
            d = [b - q * a for a, b in zip(w, p)]
            rr = total(d[0] * d[0] + d[1] * d[1])
            note_scr[...] = lanes_of(ww, wp, rr, q)
        core = meta[meta.shape[0] - 1]
        for side in range(2):
            u = d[side].astype(BF16)
            parity = core if side == 0 else 1 - core
            for z in range(pairs):
                block = u[z * HALF : (z + 1) * HALF]
                start = pl.multiple_of((2 * z + parity) * TILE, TILE)
                rows_scr[pl.ds(start, HALF), :] = block[:, :width]
                rows_scr[pl.ds(start + HALF, HALF), :] = block[:, width:]
        rows_scr[pl.ds(rows, span), :] = jnp.zeros((span, width), BF16)
        acc[...] = jnp.zeros_like(acc)

    for i in range(GROUP):
        start = pl.multiple_of(meta[step * GROUP + i], TILE)
        slab = rows_scr[pl.ds(start, span), :]
        mixed = jnp.dot(panel_ref[i], slab, preferred_element_type=F32)
        mix_scr[:, i * width : (i + 1) * width] = mixed.astype(BF16)
    acc[...] += jnp.dot(mix_scr[...], right_ref[...], preferred_element_type=F32)

    @pl.when(step == pl.num_programs(0) - 1)
    def _():
        for e in range(out_ref.shape[0]):
            cols = acc[:, e * width : (e + 1) * width]
            packed = jnp.concatenate([cols[:HALF], cols[HALF:]], axis=1)
            if turn > 0:
                before = earlier[0][e, pl.ds(0, HALF), :]
                if turn == 2:
                    q0, s0 = note_ref[0:1, 0:1], note_ref[0:1, 1:2]
                    before = s0 * (earlier[1][e, pl.ds(0, HALF), :] - q0 * before)
                packed = packed + note_scr[0:1, 3:4] * before
                out_ref[e, pl.ds(HALF, NOTE), :] = note_scr[...]
            out_ref[e, pl.ds(0, HALF), :] = packed


def apply_operator(meta, vectors, earlier, note, panels, right):
    turn = len(earlier)
    channels, tile, span = panels.shape
    full = right.shape[1]
    width = full // channels
    rows = vectors[0][0].shape[0] * 4
    whole = lambda shape: pl.BlockSpec(shape, lambda g, m: (0,) * len(shape))
    args = [half for vector in vectors for half in vector] + list(earlier)
    if turn == 2:
        args.append(note)
    in_specs = [whole(a.shape) for a in args] + [
        pl.BlockSpec((GROUP, tile, span), lambda g, m: (g, 0, 0)),
        pl.BlockSpec((GROUP * width, full), lambda g, m: (g, 0)),
    ]
    args += [panels, right]
    out_shape = (channels, HALF + (NOTE if turn else 0), 2 * width)
    return pl.pallas_call(
        functools.partial(operator_kernel, turn, rows, width),
        grid_spec=pltpu.PrefetchScalarGridSpec(
            num_scalar_prefetch=1,
            grid=(channels // GROUP,),
            in_specs=in_specs,
            out_specs=whole(out_shape),
            scratch_shapes=[
                pltpu.VMEM((rows + span, width), BF16),
                pltpu.VMEM((tile, GROUP * width), BF16),
                pltpu.VMEM((tile, full), F32),
                pltpu.VMEM((NOTE, TILE), F32),
            ],
        ),
        out_shape=jax.ShapeDtypeStruct(out_shape, F32),
        compiler_params=pltpu.CompilerParams(
            dimension_semantics=("arbitrary",), **PARAMS
        ),
        name=f"operator_{turn}",
    )(meta, *args)


def settle_kernel(entries, last, arrived_ref, p_ref, w_ref, p_out, w_out, note_out, *rest):
    _, _, energy, q = merge(arrived_ref[:, HALF, :])
    scale = lax.rsqrt(energy / entries + EPSILON)
    summed = jnp.sum(arrived_ref[:, pl.ds(0, HALF), :], axis=0)
    p = scale * (summed - q * p_ref[...])
    w = scale * (p_ref[...] - q * w_ref[...])
    p_out[...] = p
    w_out[...] = w
    note_out[...] = lanes_of(q, scale)
    if last:
        _, sums = own_sums(w, p)
        rest[0][...] = jnp.broadcast_to(lanes_of(*sums)[None], rest[0].shape)


def settle(entries, last, arrived, own_p, own_w):
    block = jax.ShapeDtypeStruct(own_p.shape, F32)
    outs = [block, block, jax.ShapeDtypeStruct((NOTE, TILE), F32)]
    if last:
        outs.append(jax.ShapeDtypeStruct((arrived.shape[0], NOTE, TILE), F32))
    return pl.pallas_call(
        functools.partial(settle_kernel, entries, last),
        in_specs=[vmem()] * 3,
        out_specs=[vmem()] * len(outs),
        out_shape=outs,
        compiler_params=pltpu.CompilerParams(**PARAMS),
        name="settle_last" if last else "settle",
    )(arrived, own_p, own_w)


def combine_kernel(got_ref, out_ref):
    note = lanes_of(*merge(got_ref[:, 0, :]))
    out_ref[...] = jnp.broadcast_to(note[None], out_ref.shape)


def combine(got, count):
    return pl.pallas_call(
        combine_kernel,
        in_specs=[vmem()],
        out_specs=vmem(),
        out_shape=jax.ShapeDtypeStruct((count, NOTE, TILE), F32),
        name="combine",
    )(got)


def finish_kernel(entries, own_ref, other_ref, w_ref, note0_ref, note1_ref, *refs):
    product_refs = refs[:ITERS]
    products_out, next_out, quotients_out = refs[ITERS:]
    notes = jnp.concatenate([own_ref[:, 0, :], other_ref[:, 0, :]], axis=0)
    _, _, energy, q = merge(notes)
    scale = lax.rsqrt(energy / entries + EPSILON)
    p = product_refs[ITERS - 1][...]
    next_out[...] = unpack(scale * (p - q * w_ref[...]))
    for n in range(ITERS):
        products_out[n] = unpack(product_refs[n][...])
    quotients_out[...] = lanes_of(note0_ref[0:1, 0:1], note1_ref[0:1, 0:1], q)


def finish(entries, own, other, w, notes, products, tile, width):
    outs = [
        jax.ShapeDtypeStruct((ITERS, tile, width), F32),
        jax.ShapeDtypeStruct((tile, width), F32),
        jax.ShapeDtypeStruct((NOTE, TILE), F32),
    ]
    args = [own, other, w, *notes, *products]
    return pl.pallas_call(
        functools.partial(finish_kernel, entries),
        in_specs=[vmem()] * len(args),
        out_specs=[vmem()] * 3,
        out_shape=outs,
        name="finish",
    )(*args)


def swap(x):
    return lax.ppermute(x, "c", [(0, 1), (1, 0)])


def exchange(x, axes):
    return lax.all_to_all(x, axes, 0, 0, tiled=True)


def gather_rows(packed):
    own = lax.all_gather(packed, "z", axis=0, tiled=True)
    return own, swap(own)


def per_device(psi, env_left, env_right, sector_tiles, pairing, coupling):
    tile, width = psi.shape
    env_count = lax.axis_size(ENV)
    z_count = lax.axis_size("z")
    full_width = width * env_count
    entries = float(tile * z_count * 2 * full_width)
    core = lax.axis_index("c")
    place = jnp.stack([lax.axis_index(("z", "c")), core, lax.axis_index(ENV)]).astype(jnp.int32)
    meta, panel, own_w = prepare(
        place, sector_tiles, pairing, coupling, env_left.reshape(tile, -1), psi
    )
    panels = lax.all_gather(panel, ENV, axis=0)
    w = gather_rows(own_w)

    part = width // 2
    held = env_right.reshape(env_count, 2, part, full_width)
    held = lax.dynamic_index_in_dim(held, core, 1, keepdims=False)
    right_own = exchange(held, ENV)
    right_other = swap(right_own)
    right = jnp.where(
        core == 0,
        jnp.stack([right_own, right_other], axis=1),
        jnp.stack([right_other, right_own], axis=1),
    ).reshape(full_width, full_width)

    sent0 = apply_operator(meta, [w], [], None, panels, right)
    p0_own = jnp.sum(exchange(sent0, ENV), axis=0)
    p0 = gather_rows(p0_own)
    sent1 = apply_operator(meta, [w, p0], [sent0], None, panels, right)
    p1_own, w1_own, note0 = settle(entries, False, exchange(sent1, ENV), p0_own, own_w)
    p1 = gather_rows(p1_own)
    sent2 = apply_operator(meta, [w, p0, p1], [sent0, sent1], note0, panels, right)
    p2_own, w2_own, note1, notes = settle(
        entries, True, exchange(sent2, ENV), p1_own, w1_own
    )
    notes = combine(exchange(notes, ENV), z_count)
    got = exchange(notes, "z")
    products, next_vector, quotients = finish(
        entries, got, swap(got), w2_own, [note0, note1], [p0_own, p1_own, p2_own], tile, width
    )
    return (products, quotients[0, :ITERS], next_vector)


def solution(mesh):
    shape = mesh.devices.shape
    fine = Mesh(mesh.devices.reshape(shape[0] // 2, 2, 4, shape[1] // 4), ("z", "c", "y", "x"))
    blk = ("z", "c")
    placed = (P(blk, ENV), P(blk, ENV, None), P(ENV, None, None), P(), P(), P())
    return jax.shard_map(
        per_device,
        mesh=fine,
        in_specs=placed,
        out_specs=(P(None, blk, ENV), P(), P(blk, ENV)),
        check_vma=False,
    )
```

```python
import functools

import jax
import jax.numpy as jnp
from jax import lax
from jax.experimental import pallas as pl
from jax.experimental.pallas import tpu as pltpu
from jax.sharding import Mesh
from jax.sharding import PartitionSpec as P

TILE = 128
HALF = TILE // 2
ITERS = 3
GROUP = 4
NOTE = 8
TAIL = 16

EPSILON = 1e-06

ENV = ("y", "x")
BF16 = jnp.bfloat16
F32 = jnp.float32
PARAMS = dict(vmem_limit_bytes=48 * 1024 * 1024)


def lanes_of(*values):
    lane = lax.broadcasted_iota(jnp.int32, (NOTE, TILE), 1)
    out = jnp.zeros((NOTE, TILE), F32)
    for i, value in enumerate(values):
        out = jnp.where(lane == i, value, out)
    return out


def total(x):
    return jnp.sum(x, keepdims=True)


def quotient_of(ww, wp):
    return jnp.where(ww > 0, wp / jnp.where(ww > 0, ww, 1.0), 0.0)


def own_sums(w, p):
    ww = total(w * w)
    wp = total(w * p)
    q = quotient_of(ww, wp)
    d = p - q * w
    return ww, wp, total(d * d), q


def write_payload(out_ref, w, p):
    q = quotient_of(total(w * w), total(w * p)).astype(BF16).astype(F32)
    out_ref[pl.ds(0, HALF), :] = (p - q * w).astype(BF16)
    out_ref[pl.ds(HALF, TAIL), :] = jnp.broadcast_to(q, (TAIL, TILE)).astype(BF16)


def merge(notes):
    ww, wp, rr, q = (notes[:, i : i + 1] for i in range(4))
    ww_all, wp_all = total(ww), total(wp)
    q_all = wp_all / ww_all
    spread = (q - q_all) * jnp.sqrt(ww)
    return ww_all, wp_all, total(rr) + total(spread * spread), q_all


def pack(block):
    return jnp.concatenate([block[:HALF], block[HALF:]], axis=1)


def unpack(packed):
    width = packed.shape[1] // 2
    return jnp.concatenate([packed[:, :width], packed[:, width:]], axis=0)


def smem():
    return pl.BlockSpec(memory_space=pltpu.SMEM)


def vmem():
    return pl.BlockSpec(memory_space=pltpu.VMEM)


def prepare_kernel(place, tiles_ref, pair_ref, couple_ref, left_ref, psi_ref,
                   meta_ref, panel_ref, packed_ref, rounded_ref, first):
    sectors, channels = pair_ref.shape
    mine, core, channel = place[0], place[1], place[2]

    def place_sector(k, carry):
        start, sector = carry
        first[k] = start
        sector = jnp.where(start <= mine, k, sector)
        return start + tiles_ref[k], sector

    _, sector = lax.fori_loop(0, sectors, place_sector, (0, 0))
    for t in range(channels):
        meta_ref[t] = first[pair_ref[sector, t]] * TILE
    meta_ref[channels] = core
    source = pair_ref[sector, channel]
    count = jnp.where(couple_ref[sector, channel] == 1, tiles_ref[source] * TILE, 0)
    column = lax.broadcasted_iota(jnp.int32, left_ref.shape, 1)
    panel_ref[...] = jnp.where(column < count, left_ref[...], jnp.zeros((), BF16))
    packed = pack(psi_ref[...].T)
    packed_ref[...] = packed
    rounded_ref[...] = packed.astype(BF16)


def prepare(place, sector_tiles, pairing, coupling, left, psi):
    channels = pairing.shape[1]
    return pl.pallas_call(
        prepare_kernel,
        in_specs=[smem()] * 4 + [vmem()] * 2,
        out_specs=[smem(), vmem(), vmem(), vmem()],
        out_shape=[
            jax.ShapeDtypeStruct((channels + 1,), jnp.int32),
            jax.ShapeDtypeStruct(left.shape, BF16),
            jax.ShapeDtypeStruct((psi.shape[1] // 2, psi.shape[0] * 2), F32),
            jax.ShapeDtypeStruct((psi.shape[1] // 2, psi.shape[0] * 2), BF16),
        ],
        scratch_shapes=[pltpu.SMEM(sector_tiles.shape, jnp.int32)],
        compiler_params=pltpu.CompilerParams(**PARAMS),
        name="prepare",
    )(place, sector_tiles, pairing, coupling, left, psi)


def operator_kernel(turn, width, *refs):
    refs = list(refs)
    meta, start_ref = refs.pop(0), refs.pop(0)
    arrived = [refs.pop(0) for _ in range(turn)]
    earlier = [refs.pop(0) for _ in range(turn)]
    note_ref = refs.pop(0) if turn == 2 else None
    panel_ref, right_ref, out_ref, rows_scr, mix_scr, acc, note_scr = refs
    step = pl.program_id(0)
    tiles = start_ref.shape[0]
    rows = tiles * TILE
    span = panel_ref.shape[2]
    wide = rows_scr.shape[1]

    def received(index):
        d = arrived[index][:, pl.ds(0, HALF), :].astype(F32)
        q = arrived[index][:, pl.ds(HALF, TAIL), :].astype(F32)[:, 0:1, 0:1]
        return d, q

    @pl.when(step == 0)
    def _():
        if turn > 0:
            w = start_ref[...].astype(F32)
            d, tile_q = received(0)
            if turn == 2:
                q0, s0 = note_ref[0:1, 0:1], note_ref[0:1, 1:2]
                w = s0[None] * (d + (tile_q - q0[None]) * w)
                d, tile_q = received(1)
            p = d + tile_q * w
            ww = total(jnp.sum(w * w, axis=0))
            wp = total(jnp.sum(w * p, axis=0))
            q = quotient_of(ww, wp)
            rest = (tile_q - q[None]) * w
            r = d + rest
            note_scr[...] = lanes_of(ww, wp, total(jnp.sum(r * r, axis=0)), q)
            rest = rest.astype(BF16)
        for k in range(tiles):
            source = start_ref if turn == 0 else arrived[turn - 1]
            block = source[k, pl.ds(0, HALF), :]
            low, high = block[:, :width], block[:, width:]
            if turn > 0:
                low = jnp.concatenate([low, rest[k][:, :width]], axis=1)
                high = jnp.concatenate([high, rest[k][:, width:]], axis=1)
            rows_scr[pl.ds(k * TILE, HALF), :] = low
            rows_scr[pl.ds(k * TILE + HALF, HALF), :] = high
        rows_scr[pl.ds(rows, span), :] = jnp.zeros((span, wide), BF16)
        acc[...] = jnp.zeros_like(acc)

    for i in range(GROUP):
        start = pl.multiple_of(meta[step * GROUP + i], TILE)
        slab = rows_scr[pl.ds(start, span), :]
        mixed = jnp.dot(panel_ref[i], slab, preferred_element_type=F32)
        if turn > 0:
            mixed = mixed[:, :width] + mixed[:, width:]
        mix_scr[:, i * width : (i + 1) * width] = mixed.astype(BF16)
    acc[...] += jnp.dot(mix_scr[...], right_ref[...], preferred_element_type=F32)

    @pl.when(step == pl.num_programs(0) - 1)
    def _():
        for e in range(out_ref.shape[0]):
            cols = acc[:, e * width : (e + 1) * width]
            packed = jnp.concatenate([cols[:HALF], cols[HALF:]], axis=1)
            if turn > 0:
                before = earlier[0][e, pl.ds(0, HALF), :]
                if turn == 2:
                    q0, s0 = note_ref[0:1, 0:1], note_ref[0:1, 1:2]
                    before = s0 * (earlier[1][e, pl.ds(0, HALF), :] - q0 * before)
                packed = packed + note_scr[0:1, 3:4] * before
                out_ref[e, pl.ds(HALF, NOTE), :] = note_scr[...]
            out_ref[e, pl.ds(0, HALF), :] = packed


def apply_operator(meta, start, arrived, earlier, note, panels, right):
    turn = len(earlier)
    channels, tile, span = panels.shape
    full = right.shape[1]
    width = full // channels
    rows = start.shape[0] * TILE
    whole = lambda shape: pl.BlockSpec(shape, lambda g, m: (0,) * len(shape))
    args = [start] + list(arrived) + list(earlier)
    if turn == 2:
        args.append(note)
    in_specs = [whole(a.shape) for a in args] + [
        pl.BlockSpec((GROUP, tile, span), lambda g, m: (g, 0, 0)),
        pl.BlockSpec((GROUP * width, full), lambda g, m: (g, 0)),
    ]
    args += [panels, right]
    out_shape = (channels, HALF + (NOTE if turn else 0), 2 * width)
    return pl.pallas_call(
        functools.partial(operator_kernel, turn, width),
        grid_spec=pltpu.PrefetchScalarGridSpec(
            num_scalar_prefetch=1,
            grid=(channels // GROUP,),
            in_specs=in_specs,
            out_specs=whole(out_shape),
            scratch_shapes=[
                pltpu.VMEM((rows + span, 2 * width if turn else width), BF16),
                pltpu.VMEM((tile, GROUP * width), BF16),
                pltpu.VMEM((tile, full), F32),
                pltpu.VMEM((NOTE, TILE), F32),
            ],
        ),
        out_shape=jax.ShapeDtypeStruct(out_shape, F32),
        compiler_params=pltpu.CompilerParams(
            dimension_semantics=("arbitrary",), **PARAMS
        ),
        name=f"operator_{turn}",
    )(meta, *args)


def open_kernel(arrived_ref, w_ref, p_out, payload_out):
    p = jnp.sum(arrived_ref[...], axis=0)
    p_out[...] = p
    write_payload(payload_out, w_ref[...], p)


def payload_shape():
    return jax.ShapeDtypeStruct((HALF + TAIL, TILE), BF16)


def open_settle(arrived, own_w):
    return pl.pallas_call(
        open_kernel,
        in_specs=[vmem()] * 2,
        out_specs=[vmem()] * 2,
        out_shape=[jax.ShapeDtypeStruct(own_w.shape, F32), payload_shape()],
        compiler_params=pltpu.CompilerParams(**PARAMS),
        name="open_settle",
    )(arrived, own_w)


def settle_kernel(entries, last, arrived_ref, p_ref, w_ref, p_out, w_out, note_out, rest_out):
    _, _, energy, q = merge(arrived_ref[:, HALF, :])
    scale = lax.rsqrt(energy / entries + EPSILON)
    summed = jnp.sum(arrived_ref[:, pl.ds(0, HALF), :], axis=0)
    p = scale * (summed - q * p_ref[...])
    w = scale * (p_ref[...] - q * w_ref[...])
    p_out[...] = p
    w_out[...] = w
    note_out[...] = lanes_of(q, scale)
    if last:
        sums = lanes_of(*own_sums(w, p))
        rest_out[...] = jnp.broadcast_to(sums[None], rest_out.shape)
    else:
        write_payload(rest_out, w, p)


def settle(entries, last, arrived, own_p, own_w):
    block = jax.ShapeDtypeStruct(own_p.shape, F32)
    outs = [block, block, jax.ShapeDtypeStruct((NOTE, TILE), F32)]
    notes = jax.ShapeDtypeStruct((arrived.shape[0], NOTE, TILE), F32)
    outs.append(notes if last else payload_shape())
    return pl.pallas_call(
        functools.partial(settle_kernel, entries, last),
        in_specs=[vmem()] * 3,
        out_specs=[vmem()] * len(outs),
        out_shape=outs,
        compiler_params=pltpu.CompilerParams(**PARAMS),
        name="settle_last" if last else "settle",
    )(arrived, own_p, own_w)


def combine_kernel(got_ref, out_ref):
    note = lanes_of(*merge(got_ref[:, 0, :]))
    out_ref[...] = jnp.broadcast_to(note[None], out_ref.shape)


def combine(got, count):
    return pl.pallas_call(
        combine_kernel,
        in_specs=[vmem()],
        out_specs=vmem(),
        out_shape=jax.ShapeDtypeStruct((count, NOTE, TILE), F32),
        name="combine",
    )(got)


def finish_kernel(entries, own_ref, other_ref, w_ref, note0_ref, note1_ref, *refs):
    product_refs = refs[:ITERS]
    products_out, next_out, quotients_out = refs[ITERS:]
    notes = jnp.concatenate([own_ref[:, 0, :], other_ref[:, 0, :]], axis=0)
    _, _, energy, q = merge(notes)
    scale = lax.rsqrt(energy / entries + EPSILON)
    p = product_refs[ITERS - 1][...]
    next_out[...] = unpack(scale * (p - q * w_ref[...])).T
    for n in range(ITERS):
        products_out[n] = unpack(product_refs[n][...]).T
    for n, value in enumerate((note0_ref[0:1, 0:1], note1_ref[0:1, 0:1], q)):
        quotients_out[n] = value[0, 0]


def finish(entries, own, other, w, notes, products, tile, width):
    outs = [
        jax.ShapeDtypeStruct((ITERS, width, tile), F32),
        jax.ShapeDtypeStruct((width, tile), F32),
        jax.ShapeDtypeStruct((ITERS,), F32),
    ]
    args = [own, other, w, *notes, *products]
    return pl.pallas_call(
        functools.partial(finish_kernel, entries),
        in_specs=[vmem()] * len(args),
        out_specs=[vmem(), vmem(), smem()],
        out_shape=outs,
        name="finish",
    )(*args)


def swap(x):
    return lax.ppermute(x, "c", [(0, 1), (1, 0)])


def exchange(x, axes):
    return lax.all_to_all(x, axes, 0, 0, tiled=True)


def gather_rows(block):
    tiles = lax.axis_size(("z", "c"))
    rows = lax.all_gather(block, ("z", "c"), axis=0, tiled=True)
    return rows.reshape((tiles,) + block.shape)


def per_device(psi, env_left, env_right, sector_tiles, pairing, coupling):
    tile, width = psi.shape
    env_count = lax.axis_size(ENV)
    z_count = lax.axis_size("z")
    full_width = width * env_count
    entries = float(tile * z_count * 2 * full_width)
    core = lax.axis_index("c")
    place = jnp.stack([lax.axis_index(("z", "c")), core, lax.axis_index(ENV)]).astype(jnp.int32)
    meta, panel, own_w, rounded = prepare(
        place, sector_tiles, pairing, coupling, env_left.reshape(tile, -1), psi.T
    )
    panels = lax.all_gather(panel, ENV, axis=0)
    start = gather_rows(rounded)

    part = width // 2
    held = env_right.reshape(env_count, 2, part, full_width)
    held = lax.dynamic_index_in_dim(held, core, 1, keepdims=False)
    right_own = exchange(held, ENV)
    right_other = swap(right_own)
    right = jnp.where(
        core == 0,
        jnp.stack([right_own, right_other], axis=1),
        jnp.stack([right_other, right_own], axis=1),
    ).reshape(full_width, full_width)

    sent0 = apply_operator(meta, start, [], [], None, panels, right)
    p0_own, payload = open_settle(exchange(sent0, ENV), own_w)
    d0 = gather_rows(payload)
    sent1 = apply_operator(meta, start, [d0], [sent0], None, panels, right)
    p1_own, w1_own, note0, payload = settle(
        entries, False, exchange(sent1, ENV), p0_own, own_w
    )
    d1 = gather_rows(payload)
    sent2 = apply_operator(meta, start, [d0, d1], [sent0, sent1], note0, panels, right)
    p2_own, w2_own, note1, notes = settle(
        entries, True, exchange(sent2, ENV), p1_own, w1_own
    )
    notes = combine(exchange(notes, ENV), z_count)
    got = exchange(notes, "z")
    products, next_vector, quotients = finish(
        entries, got, swap(got), w2_own, [note0, note1], [p0_own, p1_own, p2_own], tile, width
    )
    return (jnp.swapaxes(products, 1, 2), quotients, next_vector.T)


def solution(mesh):
    shape = mesh.devices.shape
    fine = Mesh(mesh.devices.reshape(shape[0] // 2, 2, 4, shape[1] // 4), ("z", "c", "y", "x"))
    blk = ("z", "c")
    placed = (P(blk, ENV), P(blk, ENV, None), P(ENV, None, None), P(), P(), P())
    return jax.shard_map(
        per_device,
        mesh=fine,
        in_specs=placed,
        out_specs=(P(None, blk, ENV), P(), P(blk, ENV)),
        check_vma=False,
    )
```

```python
import functools

import jax
import jax.numpy as jnp
from jax import lax
from jax.experimental import pallas as pl
from jax.experimental.pallas import tpu as pltpu
from jax.sharding import Mesh
from jax.sharding import PartitionSpec as P

TILE = 128
HALF = TILE // 2
ITERS = 3
GROUP = 8
NOTE = 8
TAIL = 16

EPSILON = 1e-06

ENV = ("y", "x")
BF16 = jnp.bfloat16
F32 = jnp.float32
PARAMS = dict(vmem_limit_bytes=48 * 1024 * 1024)


def lanes_of(*values):
    lane = lax.broadcasted_iota(jnp.int32, (NOTE, TILE), 1)
    out = jnp.zeros((NOTE, TILE), F32)
    for i, value in enumerate(values):
        out = jnp.where(lane == i, value, out)
    return out


def total(x):
    return jnp.sum(x, keepdims=True)


def quotient_of(ww, wp):
    return jnp.where(ww > 0, wp / jnp.where(ww > 0, ww, 1.0), 0.0)


def own_sums(w, p):
    ww = total(w * w)
    wp = total(w * p)
    q = quotient_of(ww, wp)
    d = p - q * w
    return ww, wp, total(d * d), q


def write_payload(out_ref, w, p):
    q = quotient_of(total(w * w), total(w * p)).astype(BF16).astype(F32)
    out_ref[pl.ds(0, HALF), :] = (p - q * w).astype(BF16)
    out_ref[pl.ds(HALF, TAIL), :] = jnp.broadcast_to(q, (TAIL, TILE)).astype(BF16)


def merge(notes):
    ww, wp, rr, q = (notes[:, i : i + 1] for i in range(4))
    ww_all, wp_all = total(ww), total(wp)
    q_all = wp_all / ww_all
    spread = (q - q_all) * jnp.sqrt(ww)
    return ww_all, wp_all, total(rr) + total(spread * spread), q_all


def pack(block):
    return jnp.concatenate([block[:HALF], block[HALF:]], axis=1)


def unpack(packed):
    width = packed.shape[1] // 2
    return jnp.concatenate([packed[:, :width], packed[:, width:]], axis=0)


def smem():
    return pl.BlockSpec(memory_space=pltpu.SMEM)


def vmem():
    return pl.BlockSpec(memory_space=pltpu.VMEM)


def prepare_kernel(place, tiles_ref, pair_ref, couple_ref, left_ref, psi_ref,
                   meta_ref, panel_ref, packed_ref, rounded_ref, first):
    sectors, channels = pair_ref.shape
    mine, core, channel = place[0], place[1], place[2]

    def place_sector(k, carry):
        start, sector = carry
        first[k] = start
        sector = jnp.where(start <= mine, k, sector)
        return start + tiles_ref[k], sector

    _, sector = lax.fori_loop(0, sectors, place_sector, (0, 0))
    for t in range(channels):
        meta_ref[t] = first[pair_ref[sector, t]] * TILE
    meta_ref[channels] = core
    source = pair_ref[sector, channel]
    count = jnp.where(couple_ref[sector, channel] == 1, tiles_ref[source] * TILE, 0)
    column = lax.broadcasted_iota(jnp.int32, left_ref.shape, 1)
    panel_ref[...] = jnp.where(column < count, left_ref[...], jnp.zeros((), BF16))
    packed = pack(psi_ref[...].T)
    packed_ref[...] = packed
    rounded_ref[...] = packed.astype(BF16)


def prepare(place, sector_tiles, pairing, coupling, left, psi):
    channels = pairing.shape[1]
    return pl.pallas_call(
        prepare_kernel,
        in_specs=[smem()] * 4 + [vmem()] * 2,
        out_specs=[smem(), vmem(), vmem(), vmem()],
        out_shape=[
            jax.ShapeDtypeStruct((channels + 1,), jnp.int32),
            jax.ShapeDtypeStruct(left.shape, BF16),
            jax.ShapeDtypeStruct((psi.shape[1] // 2, psi.shape[0] * 2), F32),
            jax.ShapeDtypeStruct((psi.shape[1] // 2, psi.shape[0] * 2), BF16),
        ],
        scratch_shapes=[pltpu.SMEM(sector_tiles.shape, jnp.int32)],
        compiler_params=pltpu.CompilerParams(**PARAMS),
        name="prepare",
    )(place, sector_tiles, pairing, coupling, left, psi)


def operator_kernel(turn, width, *refs):
    refs = list(refs)
    meta, start_ref = refs.pop(0), refs.pop(0)
    arrived = [refs.pop(0) for _ in range(turn)]
    earlier = [refs.pop(0) for _ in range(turn)]
    note_ref = refs.pop(0) if turn == 2 else None
    panels_ref, right_ref, out_ref, rows_scr, panel_ref, mix_scr, acc, note_scr, sems = refs
    channels = panel_ref.shape[0]
    tiles = start_ref.shape[0]
    rows = tiles * TILE
    span = panel_ref.shape[2]
    wide = rows_scr.shape[1]

    def received(index):
        d = arrived[index][:, pl.ds(0, HALF), :].astype(F32)
        q = arrived[index][:, pl.ds(HALF, TAIL), :].astype(F32)[:, 0:1, 0:1]
        return d, q

    copies = []
    for g in range(channels // GROUP):
        part = pl.ds(g * GROUP, GROUP)
        copies.append(
            pltpu.make_async_copy(panels_ref.at[part], panel_ref.at[part], sems.at[g])
        )
        copies[g].start()

    if turn > 0:
        w = start_ref[...].astype(F32)
        d, tile_q = received(0)
        if turn == 2:
            q0, s0 = note_ref[0:1, 0:1], note_ref[0:1, 1:2]
            w = s0[None] * (d + (tile_q - q0[None]) * w)
            d, tile_q = received(1)
        p = d + tile_q * w
        ww = total(jnp.sum(w * w, axis=0))
        wp = total(jnp.sum(w * p, axis=0))
        q = quotient_of(ww, wp)
        rest = (tile_q - q[None]) * w
        r = d + rest
        note_scr[...] = lanes_of(ww, wp, total(jnp.sum(r * r, axis=0)), q)
        rest = rest.astype(BF16)
    for k in range(tiles):
        source = start_ref if turn == 0 else arrived[turn - 1]
        block = source[k, pl.ds(0, HALF), :]
        low, high = block[:, :width], block[:, width:]
        if turn > 0:
            low = jnp.concatenate([low, rest[k][:, :width]], axis=1)
            high = jnp.concatenate([high, rest[k][:, width:]], axis=1)
        rows_scr[pl.ds(k * TILE, HALF), :] = low
        rows_scr[pl.ds(k * TILE + HALF, HALF), :] = high
    rows_scr[pl.ds(rows, span), :] = jnp.zeros((span, wide), BF16)

    for t in range(channels):
        if t % GROUP == 0:
            copies[t // GROUP].wait()
        start = pl.multiple_of(meta[t], TILE)
        slab = rows_scr[pl.ds(start, span), :]
        mixed = jnp.dot(panel_ref[t], slab, preferred_element_type=F32)
        if turn > 0:
            mixed = mixed[:, :width] + mixed[:, width:]
        mix_scr[:, t * width : (t + 1) * width] = mixed.astype(BF16)
    acc[...] = jnp.dot(mix_scr[...], right_ref[...], preferred_element_type=F32)

    for e in range(out_ref.shape[0]):
        cols = acc[:, e * width : (e + 1) * width]
        packed = jnp.concatenate([cols[:HALF], cols[HALF:]], axis=1)
        if turn > 0:
            before = earlier[0][e, pl.ds(0, HALF), :]
            if turn == 2:
                q0, s0 = note_ref[0:1, 0:1], note_ref[0:1, 1:2]
                before = s0 * (earlier[1][e, pl.ds(0, HALF), :] - q0 * before)
            packed = packed + note_scr[0:1, 3:4] * before
            out_ref[e, pl.ds(HALF, NOTE), :] = note_scr[...]
        out_ref[e, pl.ds(0, HALF), :] = packed


def apply_operator(meta, start, arrived, earlier, note, panels, right):
    turn = len(earlier)
    channels, tile, span = panels.shape
    full = right.shape[1]
    width = full // channels
    rows = start.shape[0] * TILE
    args = [start] + list(arrived) + list(earlier)
    if turn == 2:
        args.append(note)
    out_shape = (channels, HALF + (NOTE if turn else 0), 2 * width)
    return pl.pallas_call(
        functools.partial(operator_kernel, turn, width),
        in_specs=[smem()] + [vmem()] * len(args) + [pl.BlockSpec(memory_space=pl.ANY), vmem()],
        out_specs=vmem(),
        scratch_shapes=[
            pltpu.VMEM((rows + span, 2 * width if turn else width), BF16),
            pltpu.VMEM(panels.shape, BF16),
            pltpu.VMEM((tile, full), BF16),
            pltpu.VMEM((tile, full), F32),
            pltpu.VMEM((NOTE, TILE), F32),
            pltpu.SemaphoreType.DMA((channels // GROUP,)),
        ],
        out_shape=jax.ShapeDtypeStruct(out_shape, F32),
        compiler_params=pltpu.CompilerParams(**PARAMS),
        name=f"operator_{turn}",
    )(meta, *args, panels, right)


def open_kernel(arrived_ref, w_ref, p_out, payload_out):
    p = jnp.sum(arrived_ref[...], axis=0)
    p_out[...] = p
    write_payload(payload_out, w_ref[...], p)


def payload_shape():
    return jax.ShapeDtypeStruct((HALF + TAIL, TILE), BF16)


def open_settle(arrived, own_w):
    return pl.pallas_call(
        open_kernel,
        in_specs=[vmem()] * 2,
        out_specs=[vmem()] * 2,
        out_shape=[jax.ShapeDtypeStruct(own_w.shape, F32), payload_shape()],
        compiler_params=pltpu.CompilerParams(**PARAMS),
        name="open_settle",
    )(arrived, own_w)


def settle_kernel(entries, last, arrived_ref, p_ref, w_ref, p_out, w_out, note_out, rest_out):
    _, _, energy, q = merge(arrived_ref[:, HALF, :])
    scale = lax.rsqrt(energy / entries + EPSILON)
    summed = jnp.sum(arrived_ref[:, pl.ds(0, HALF), :], axis=0)
    p = scale * (summed - q * p_ref[...])
    w = scale * (p_ref[...] - q * w_ref[...])
    p_out[...] = p
    w_out[...] = w
    note_out[...] = lanes_of(q, scale)
    if last:
        sums = lanes_of(*own_sums(w, p))
        rest_out[...] = jnp.broadcast_to(sums[None], rest_out.shape)
    else:
        write_payload(rest_out, w, p)


def settle(entries, last, arrived, own_p, own_w):
    block = jax.ShapeDtypeStruct(own_p.shape, F32)
    outs = [block, block, jax.ShapeDtypeStruct((NOTE, TILE), F32)]
    notes = jax.ShapeDtypeStruct((arrived.shape[0], NOTE, TILE), F32)
    outs.append(notes if last else payload_shape())
    return pl.pallas_call(
        functools.partial(settle_kernel, entries, last),
        in_specs=[vmem()] * 3,
        out_specs=[vmem()] * len(outs),
        out_shape=outs,
        compiler_params=pltpu.CompilerParams(**PARAMS),
        name="settle_last" if last else "settle",
    )(arrived, own_p, own_w)


def combine_kernel(got_ref, out_ref):
    note = lanes_of(*merge(got_ref[:, 0, :]))
    out_ref[...] = jnp.broadcast_to(note[None], out_ref.shape)


def combine(got, count):
    return pl.pallas_call(
        combine_kernel,
        in_specs=[vmem()],
        out_specs=vmem(),
        out_shape=jax.ShapeDtypeStruct((count, NOTE, TILE), F32),
        name="combine",
    )(got)


def finish_kernel(entries, own_ref, other_ref, w_ref, note0_ref, note1_ref, *refs):
    product_refs = refs[:ITERS]
    products_out, next_out, quotients_out = refs[ITERS:]
    notes = jnp.concatenate([own_ref[:, 0, :], other_ref[:, 0, :]], axis=0)
    _, _, energy, q = merge(notes)
    scale = lax.rsqrt(energy / entries + EPSILON)
    p = product_refs[ITERS - 1][...]
    next_out[...] = unpack(scale * (p - q * w_ref[...])).T
    for n in range(ITERS):
        products_out[n] = unpack(product_refs[n][...]).T
    for n, value in enumerate((note0_ref[0:1, 0:1], note1_ref[0:1, 0:1], q)):
        quotients_out[n] = value[0, 0]


def finish(entries, own, other, w, notes, products, tile, width):
    outs = [
        jax.ShapeDtypeStruct((ITERS, width, tile), F32),
        jax.ShapeDtypeStruct((width, tile), F32),
        jax.ShapeDtypeStruct((ITERS,), F32),
    ]
    args = [own, other, w, *notes, *products]
    return pl.pallas_call(
        functools.partial(finish_kernel, entries),
        in_specs=[vmem()] * len(args),
        out_specs=[vmem(), vmem(), smem()],
        out_shape=outs,
        name="finish",
    )(*args)


def swap(x):
    return lax.ppermute(x, "c", [(0, 1), (1, 0)])


def exchange(x, axes):
    return lax.all_to_all(x, axes, 0, 0, tiled=True)


def gather_rows(block):
    tiles = lax.axis_size(("z", "c"))
    rows = lax.all_gather(block, ("z", "c"), axis=0, tiled=True)
    return rows.reshape((tiles,) + block.shape)


def per_device(psi, env_left, env_right, sector_tiles, pairing, coupling):
    tile, width = psi.shape
    env_count = lax.axis_size(ENV)
    z_count = lax.axis_size("z")
    full_width = width * env_count
    entries = float(tile * z_count * 2 * full_width)
    core = lax.axis_index("c")
    place = jnp.stack([lax.axis_index(("z", "c")), core, lax.axis_index(ENV)]).astype(jnp.int32)
    meta, panel, own_w, rounded = prepare(
        place, sector_tiles, pairing, coupling, env_left.reshape(tile, -1), psi.T
    )
    panels = lax.all_gather(panel, ENV, axis=0)
    start = gather_rows(rounded)

    part = width // 2
    held = env_right.reshape(env_count, 2, part, full_width)
    held = lax.dynamic_index_in_dim(held, core, 1, keepdims=False)
    right_own = exchange(held, ENV)
    right_other = swap(right_own)
    right = jnp.where(
        core == 0,
        jnp.stack([right_own, right_other], axis=1),
        jnp.stack([right_other, right_own], axis=1),
    ).reshape(full_width, full_width)

    sent0 = apply_operator(meta, start, [], [], None, panels, right)
    p0_own, payload = open_settle(exchange(sent0, ENV), own_w)
    d0 = gather_rows(payload)
    sent1 = apply_operator(meta, start, [d0], [sent0], None, panels, right)
    p1_own, w1_own, note0, payload = settle(
        entries, False, exchange(sent1, ENV), p0_own, own_w
    )
    d1 = gather_rows(payload)
    sent2 = apply_operator(meta, start, [d0, d1], [sent0, sent1], note0, panels, right)
    p2_own, w2_own, note1, notes = settle(
        entries, True, exchange(sent2, ENV), p1_own, w1_own
    )
    notes = combine(exchange(notes, ENV), z_count)
    got = exchange(notes, "z")
    products, next_vector, quotients = finish(
        entries, got, swap(got), w2_own, [note0, note1], [p0_own, p1_own, p2_own], tile, width
    )
    return (jnp.swapaxes(products, 1, 2), quotients, next_vector.T)


def solution(mesh):
    shape = mesh.devices.shape
    fine = Mesh(mesh.devices.reshape(shape[0] // 2, 2, 4, shape[1] // 4), ("z", "c", "y", "x"))
    blk = ("z", "c")
    placed = (P(blk, ENV), P(blk, ENV, None), P(ENV, None, None), P(), P(), P())
    return jax.shard_map(
        per_device,
        mesh=fine,
        in_specs=placed,
        out_specs=(P(None, blk, ENV), P(), P(blk, ENV)),
        check_vma=False,
    )
```
